32 devices in a mesh: tile: 8 (over z, x), ka: 4 (over y, core).
Axes of the slice: x: 2, y: 2, z: 4, core: 2. Of those that a mesh axis runs over, the one named last changes fastest.
Arguments:
- amplitudes: bfloat16 [128, 32, 512], P(('tile', 'ka')), may hold values from -6 to 6
- integrals: bfloat16 [64, 512, 4096], P('tile', None, 'ka'), may hold values from -0.046875 to 0.046875
- slot_block: int32 [64], replicated, may hold values from 0 to 32, as said below
- rest: bfloat16 [128, 4096], P('tile', 'ka'), may hold values from -12 to 12
- occ_energy: float32 [128], P('tile'), may hold values from -2 to -0.5
- vir_energy: float32 [4096], P('ka'), may hold values from 0.5 to 3
Outputs:
- new_amp: bfloat16 [128, 4096], P('tile', 'ka')
The draws below stay inside these ranges and needn't reach their ends.
Inputs may be any that keep to these rules, and one draw needn't show every extreme that they name: `slot_block`: each of the 32 blocks is stored in exactly one slot; the value 32 marks an empty slot. Slots s*8 to s*8 + 7 belong to owner s along tile; an owner holds 0 to 8 blocks, and some owner holds exactly 8.
All inputs are finite; a program needn't handle non-finite values.
Results may differ from the reference program's by a relative error of at most 0.001.
Values may be sent and summed in bfloat16 or wider, within the bound.
A program may use at most 128 MiB of HBM per device.

```python
import jax
import jax.numpy as jnp
from jax import lax

BW = 512
CAP = 8
NBLK = 32
SLOTS = 64
ROWS = 128
PAIRS = 4096


def draw_slot_block(key, part):
    tile_count = SLOTS // CAP
    half_count = tile_count // 2
    sub_keys = jax.random.split(key, 4)
    firsts = jax.random.randint(sub_keys[0], (half_count,), 0, CAP + 1)
    firsts = firsts.at[0].set(CAP)
    counts = jnp.concatenate([firsts, CAP - firsts])
    counts = counts[jax.random.permutation(sub_keys[1], tile_count)]
    orders = jax.vmap(lambda sub_key: jax.random.permutation(sub_key, CAP))(jax.random.split(sub_keys[2], tile_count))
    is_live = (orders < counts[:, None]).reshape(-1)
    live_rank = jnp.cumsum(is_live.astype(jnp.int32)) - 1
    block_ids = jax.random.permutation(sub_keys[3], NBLK).astype(jnp.int32)
    chosen = block_ids[jnp.clip(live_rank, 0, NBLK - 1)]
    return jnp.where(is_live, chosen, NBLK).astype(jnp.int32)


def shard_levels(key, extent, pieces, least, high):
    gain, own = 1.0, jax.random.fold_in(key, 6)
    for dim, blocks in pieces:
        draws = jnp.exp(jax.random.uniform(jax.random.fold_in(own, dim), (blocks,), jnp.float32, least / len(pieces), high / len(pieces)))
        gain = gain * jnp.repeat(draws, extent[dim] // blocks).reshape([-1 if axis == dim else 1 for axis in range(len(extent))])
    return gain


def noise(key, shape, deviation, most, pieces=(), kind=jnp.bfloat16):
    gain = shard_levels(key, shape, pieces, -0.22, 0.18) if pieces else 1.0
    array = jax.random.normal(key, shape, jnp.float32) * deviation * gain
    return jnp.minimum(jnp.maximum(array, -most), most).astype(kind)


def setup_inputs(seed: int = 0) -> dict:
    keys = jax.random.split(jax.random.key(seed), 7)
    amplitudes = noise(keys[0], (ROWS, NBLK, BW), 1.0, 6.0, ((0, 32),))
    integrals = noise(keys[1], (SLOTS, BW, PAIRS), (NBLK * BW) ** -0.5, 0.046875, ((0, 8), (2, 4)))
    slot_block = draw_slot_block(jax.random.fold_in(keys[6], 71), 0)
    rest = noise(keys[3], (ROWS, PAIRS), 2.0, 12.0, ((0, 8), (1, 4)))
    occ_energy = jnp.clip(-2.0 + 1.5 * jax.random.uniform(keys[4], (ROWS,), jnp.float32) ** shard_levels(keys[4], (ROWS,), ((0, 8),), -0.2, 0.2), -2.0, -0.5)
    vir_energy = jnp.clip(0.5 + 2.5 * jax.random.uniform(keys[5], (PAIRS,), jnp.float32) ** shard_levels(keys[5], (PAIRS,), ((0, 4),), -0.2, 0.2), 0.5, 3.0)
    return dict(amplitudes=amplitudes, integrals=integrals, slot_block=slot_block, rest=rest, occ_energy=occ_energy, vir_energy=vir_energy)


def reference(amplitudes, integrals, slot_block, rest, occ_energy, vir_energy):
    slot_of = jnp.zeros((NBLK + 1,), jnp.int32).at[slot_block].set(jnp.arange(SLOTS, dtype=jnp.int32))

    def add_block(position, running):
        amp_block = lax.dynamic_index_in_dim(amplitudes, position, 1, keepdims=False)
        int_slab = lax.dynamic_index_in_dim(integrals, slot_of[position], 0, keepdims=False)
        return running + jnp.dot(amp_block, int_slab, preferred_element_type=jnp.float32)

    ladder = lax.fori_loop(0, NBLK, add_block, jnp.zeros((ROWS, PAIRS), jnp.float32))
    denominator = vir_energy[None, :] - occ_energy[:, None]
    return ((rest.astype(jnp.float32) + ladder) / denominator).astype(jnp.bfloat16)
```

```python
import functools

import jax
import jax.numpy as jnp
from jax import lax
from jax.experimental import pallas as pl
from jax.experimental.pallas import tpu as pltpu
from jax.sharding import PartitionSpec as P

MESH = pl.DeviceIdType.MESH
UNROLL = 8


def repeat(count, body):
    if count <= UNROLL:
        for index in range(count):
            body(index)
    else:
        pl.loop(0, count)(body)


def kernel(tiles, fan, chunks, slots_ref, amp_ref, rest_ref, occ_ref, vir_ref, int_ref, out_ref,
           wide, outgoing, arrived, lhs_peer, lhs_own, blocks, pair_send, pair_recv, line_send, line_recv,
           int_sem, self_sem, direct_sem, recv_sem, fwd_sem, pair_sem, pair_rsem, line_sem, line_rsem):
    me, k = lax.axis_index("tile"), lax.axis_index("ka")
    rows, nblocks, width = amp_ref.shape
    capacity = int_ref.shape[0]
    half = tiles // 2
    group = fan * rows
    span = out_ref.shape[1] // chunks

    fills = [pltpu.make_async_copy(int_ref.at[s], blocks.at[s], int_sem.at[s]) for s in range(capacity)]

    barrier = pltpu.get_barrier_semaphore()

    def greet(m):
        pl.semaphore_signal(barrier, inc=1, device_id={"tile": me ^ m}, device_id_type=MESH)

    repeat(tiles - 1, lambda i: greet(i + 1))
    bits = []
    bit = fan // 2
    while bit:
        bits.append(bit)
        bit //= 2
    for bit in bits:
        pl.semaphore_signal(barrier, inc=1, device_id={"ka": k ^ bit}, device_id_type=MESH)
    for fill in fills:
        fill.start()

    for r in range(rows):
        for lane in range(width // 128):
            part = amp_ref[r, :, pl.ds(lane * 128, 128)].astype(jnp.float32)
            wide[lane, pl.ds(r * nblocks, nblocks), :] = part

    def gather(m):
        for s in range(capacity):
            block = slots_ref[(me ^ m) * capacity + s]
            start = jnp.minimum(block, nblocks - 1)
            for lane in range(width // 128):
                picked = wide[lane, pl.ds(start, rows, stride=nblocks), :]
                picked = jnp.where(block < nblocks, picked, 0.0)
                outgoing[m, :, pl.ds(s * width + lane * 128, 128)] = picked.astype(jnp.bfloat16)

    repeat(tiles, gather)
    pl.semaphore_wait(barrier, tiles - 1 + len(bits))

    def direct(m):
        return pltpu.make_async_remote_copy(
            src_ref=outgoing.at[m], dst_ref=arrived.at[m, k], send_sem=direct_sem.at[m],
            recv_sem=recv_sem.at[m, 0], device_id={"tile": me ^ m}, device_id_type=MESH)

    def forward(m, q, bit, own=False):
        source = outgoing.at[m] if own else arrived.at[m, k ^ q]
        return pltpu.make_async_remote_copy(
            src_ref=source, dst_ref=arrived.at[m, k ^ q], send_sem=fwd_sem.at[m, q | bit],
            recv_sem=recv_sem.at[m, q | bit], device_id={"ka": k ^ bit}, device_id_type=MESH)

    keep = pltpu.make_async_copy(outgoing.at[0], arrived.at[0, k], self_sem)
    keep.start()

    def spread(m, own=False):
        for bit in bits:
            forward(m, 0, bit, own).start()

    def relay(m):
        for high in range(len(bits) - 1):
            top = bits[high]
            for rest_q in range(0, fan, 2 * top):
                q = rest_q | top
                forward_wait(m, q)
                for bit in bits[high + 1:]:
                    forward(m, q, bit).start()

    def forward_wait(m, q):
        pltpu.make_async_remote_copy(
            src_ref=arrived.at[m, k], dst_ref=arrived.at[m, k], send_sem=fwd_sem.at[m, q],
            recv_sem=recv_sem.at[m, q], device_id={"ka": k ^ 1}, device_id_type=MESH).wait_recv()

    spread(0, own=True)
    repeat(half, lambda i: direct(tiles - 1 - 2 * i).start())
    repeat(half - 1, lambda i: direct(tiles - 2 - 2 * i).start())

    def take(m):
        direct(m).wait_recv()
        spread(m)

    def step_peer(i):
        take(tiles - 1 - 2 * i)

    repeat(half, step_peer)
    relay(0)

    def step_own(i):
        relay(tiles - 1 - 2 * i)
        take(tiles - 2 - 2 * i)

    repeat(half - 1, step_own)
    relay(1)
    repeat(half - 1, lambda i: relay(tiles - 2 - 2 * i))

    def finish(m):
        for q in range(1, fan):
            if q & 1:
                forward_wait(m, q)

    def assemble(m, target, j):
        pieces = [arrived[m, q].astype(jnp.float32) for q in range(fan)]
        target[pl.ds(j * group, group), :] = jnp.concatenate(pieces, axis=0).astype(jnp.bfloat16)

    def ready_peer(i):
        m = tiles - 1 - 2 * i
        finish(m)
        assemble(m, lhs_peer, half - 1 - i)

    repeat(half, ready_peer)
    for fill in fills:
        fill.wait()

    total = half * group
    piece = min(total, 128)

    def product(source, c, base):
        acc = None
        for s in range(capacity):
            term = jnp.dot(source[pl.ds(base, piece), pl.ds(s * width, width)],
                           blocks[s, :, pl.ds(c * span, span)], preferred_element_type=jnp.float32)
            acc = term if acc is None else acc + term
        return acc

    def pair(c):
        return pltpu.make_async_remote_copy(
            src_ref=pair_send.at[c], dst_ref=pair_recv.at[c], send_sem=pair_sem.at[c],
            recv_sem=pair_rsem.at[c], device_id={"tile": me ^ 1}, device_id_type=MESH)

    def line(c, j):
        return pltpu.make_async_remote_copy(
            src_ref=line_send.at[c, pl.ds(j * group, group)], dst_ref=line_recv.at[c, j],
            send_sem=line_sem.at[c, j], recv_sem=line_rsem.at[c, j],
            device_id={"tile": me ^ (2 * j)}, device_id_type=MESH)

    for c in range(chunks):
        def fill_pair(b):
            base = b * piece
            pair_send[c, pl.ds(base, piece), :] = product(lhs_peer, c, base)
        repeat(total // piece, fill_pair)
        pair(c).start()

    keep.wait()
    for q in range(1, fan):
        if q & 1:
            forward_wait(0, q)
    assemble(0, lhs_own, 0)

    def ready_own(i):
        m = tiles - 2 - 2 * i
        finish(m)
        assemble(m, lhs_own, half - 1 - i)

    repeat(half - 1, ready_own)

    for c in range(chunks):
        def fill_line(b):
            base = b * piece
            line_send[c, pl.ds(base, piece), :] = product(lhs_own, c, base)
        repeat(total // piece, fill_line)
        pair(c).wait_recv()

        def add_line(b):
            base = b * piece
            line_send[c, pl.ds(base, piece), :] += pair_recv[c, pl.ds(base, piece), :]
        repeat(total // piece, add_line)
        repeat(half - 1, lambda i: line(c, half - 1 - i).start())

    eye = lax.broadcasted_iota(jnp.int32, (group, group), 0) == lax.broadcasted_iota(jnp.int32, (group, group), 1)
    occ = jnp.sum(jnp.where(eye, occ_ref[...], 0.0), axis=1, keepdims=True)
    for c in range(chunks):
        columns = pl.ds(c * span, span)
        ladder = line_send[c, pl.ds(0, group), :]
        for j in range(1, half):
            line(c, j).wait_recv()
            ladder = ladder + line_recv[c, j]
        value = rest_ref[:, columns].astype(jnp.float32) + ladder
        out_ref[:, columns] = (value / (vir_ref[:, columns] - occ)).astype(out_ref.dtype)

    repeat(tiles - 1, lambda i: direct(i + 1).wait_send())

    def drain(m):
        for q in range(1, fan):
            pltpu.make_async_remote_copy(
                src_ref=arrived.at[m, k], dst_ref=arrived.at[m, k], send_sem=fwd_sem.at[m, q],
                recv_sem=recv_sem.at[m, q], device_id={"ka": k ^ 1}, device_id_type=MESH).wait_send()

    repeat(tiles, drain)
    for c in range(chunks):
        pair(c).wait_send()
        repeat(half - 1, lambda i: line(c, i + 1).wait_send())


def per_device(tiles, fan, amplitudes, integrals, slot_block, rest, occ_energy, vir_energy):
    rows, nblocks, width = amplitudes.shape
    capacity, _, columns = integrals.shape
    half, group = tiles // 2, fan * rows
    chunks = 4
    span = columns // chunks
    vmem = pl.BlockSpec(memory_space=pltpu.VMEM)
    f32, bf16 = jnp.float32, jnp.bfloat16
    dma = pltpu.SemaphoreType.DMA
    return pl.pallas_call(
        functools.partial(kernel, tiles, fan, chunks),
        out_shape=jax.ShapeDtypeStruct(rest.shape, bf16),
        in_specs=[pl.BlockSpec(memory_space=pltpu.SMEM), vmem, vmem, vmem, vmem, pl.BlockSpec(memory_space=pl.ANY)],
        out_specs=vmem,
        scratch_shapes=[
            pltpu.VMEM((width // 128, rows * nblocks, 128), f32),
            pltpu.VMEM((tiles, rows, capacity * width), bf16),
            pltpu.VMEM((tiles, fan, rows, capacity * width), bf16),
            pltpu.VMEM((half * group, capacity * width), bf16),
            pltpu.VMEM((half * group, capacity * width), bf16),
            pltpu.VMEM((capacity, width, columns), bf16),
            pltpu.VMEM((chunks, half * group, span), f32),
            pltpu.VMEM((chunks, half * group, span), f32),
            pltpu.VMEM((chunks, half * group, span), f32),
            pltpu.VMEM((chunks, half, group, span), f32),
            dma((capacity,)),
            dma,
            dma((tiles,)),
            dma((tiles, fan)),
            dma((tiles, fan)),
            dma((chunks,)),
            dma((chunks,)),
            dma((chunks, half)),
            dma((chunks, half)),
        ],
        compiler_params=pltpu.CompilerParams(
            collective_id=0, has_side_effects=True, vmem_limit_bytes=60 * 1024 * 1024),
    )(slot_block, amplitudes, rest, occ_energy.reshape(1, -1), vir_energy.reshape(1, -1), integrals)


def solution(mesh):
    in_specs = (
        P(("tile", "ka"), None, None),
        P("tile", None, "ka"),
        P(),
        P("tile", "ka"),
        P("tile"),
        P("ka"),
    )
    body = functools.partial(per_device, mesh.shape["tile"], mesh.shape["ka"])
    return jax.shard_map(body, mesh=mesh, in_specs=in_specs, out_specs=P("tile", "ka"), check_vma=False)
```
